128 devices in a mesh: tm: 4 (over y_hi, core), inputs: 32 (over z, y_lo, x).
Axes of the slice: x: 4, y: 4 (y_hi: 2, y_lo: 2; y = y_hi * 2 + y_lo), z: 4, core: 2. Of those that a mesh axis runs over, the one named last changes fastest.
Arguments:
- voltages: bfloat16 [512, 524288], P('inputs', 'tm'), may hold values from -6 to 6
- filter_taps: float32 [4, 512], replicated, may hold values from -3 to 3
Outputs:
- visibility: float32 [4, 256, 2, 512, 512], P(None, ('tm', 'inputs'))
The draws below stay inside these ranges and needn't reach their ends.
All inputs are finite; a program needn't handle non-finite values.
Results may differ from the reference program's by a relative error of at most 0.0059.
Values may be sent and summed in bfloat16 or wider, within the bound.
No kernel may reach another device: no remote copies, remote signals or barrier semaphores. Data moves between devices by JAX's collectives and lax.ppermute only.
A program may use at most 128 MiB of HBM per device.

```python
import math
import jax
import jax.numpy as jnp
from jax import lax

NIN = 512
NFFT = 512
TAPS = 4
SPEC = 256
DUMPS = 4
SAMPLES = 524288


def shard_levels(rng, extent, cuts, smallest, largest):
    level = 1.0
    for axis_at, blocks in cuts:
        draws = jax.random.uniform(jax.random.fold_in(jax.random.fold_in(rng, 6), axis_at), (blocks,), jnp.float32, smallest / len(cuts), largest / len(cuts))
        level = level * jnp.repeat(jnp.exp(draws), extent[axis_at] // blocks).reshape((-1,) + (1,) * (len(extent) - 1 - axis_at))
    return level


def bell_draw(key, shape, spread, reach, pieces=(), kind=jnp.bfloat16):
    level = shard_levels(key, shape, pieces, -0.22, 0.18) if pieces else 1.0
    values = jax.random.normal(key, shape, jnp.float32) * spread * level
    return jnp.minimum(jnp.maximum(values, -reach), reach).astype(kind)


def setup_inputs(seed: int = 0) -> dict:
    key_of = jax.random.split(jax.random.key(seed), 3)
    return {
        "voltages": bell_draw(key_of[0], (NIN, SAMPLES), 1.0, 6.0, ((0, 32), (1, 4))),
        "filter_taps": bell_draw(key_of[1], (TAPS, NFFT), 0.5, 3.0, (), jnp.float32),
    }


def fourier_table():
    rows = lax.broadcasted_iota(jnp.int32, (NFFT, NFFT // 2), 0)
    cols = lax.broadcasted_iota(jnp.int32, (NFFT, NFFT // 2), 1)
    phase = (rows * cols % NFFT).astype(jnp.float32) * (2.0 * math.pi / NFFT)
    factor = 1.0 / math.sqrt(NFFT)
    return jnp.stack([jnp.cos(phase) * factor, -jnp.sin(phase) * factor], axis=1).astype(jnp.bfloat16)

def reference(voltages, filter_taps):
    spectra_count = DUMPS * SPEC
    blocks = voltages.reshape(NIN, spectra_count, NFFT)
    padded = jnp.concatenate([jnp.zeros((NIN, TAPS - 1, NFFT), voltages.dtype), blocks], axis=1)
    flat_table = fourier_table().reshape(NFFT, NFFT)

    def channelize(samples):
        running = jnp.zeros((spectra_count, NFFT), jnp.float32)
        for tap_index in range(TAPS):
            running = running + filter_taps[tap_index][None, :] * samples[tap_index:tap_index + spectra_count].astype(jnp.float32)
        filtered = running.astype(jnp.bfloat16)
        return jnp.dot(filtered, flat_table, preferred_element_type=jnp.float32).astype(jnp.bfloat16)
    spectra = lax.map(channelize, padded)
    ordered = spectra.reshape(NIN, DUMPS, SPEC, 2, NFFT // 2).transpose(1, 4, 0, 3, 2)

    def correlate(channel_data):
        values = channel_data.astype(jnp.float32)
        real_part = values[:, 0, :]
        imag_part = values[:, 1, :]
        best = lax.Precision.HIGHEST
        real_sum = jnp.dot(real_part, real_part.T, precision=best) + jnp.dot(imag_part, imag_part.T, precision=best)
        imag_sum = jnp.dot(imag_part, real_part.T, precision=best) - jnp.dot(real_part, imag_part.T, precision=best)
        return jnp.stack([real_sum, imag_sum]) / SPEC

    def per_dump(dump_data):
        return lax.map(correlate, dump_data)
    return lax.map(per_dump, ordered)
```

```python
import math

import jax
import jax.numpy as jnp
import ml_dtypes
import numpy as np
from jax import lax
from jax.experimental import pallas as pl
from jax.experimental.pallas import tpu as pltpu
from jax.sharding import PartitionSpec as P

NFFT = 512
TAPS = 4
CHANNELS = NFFT // 2
LANES = 128
GROUP = 16


def fourier_rows():
    n = np.arange(NFFT)
    k = np.arange(CHANNELS)
    phase = (k[:, None] * n[None, :] % NFFT) * (2.0 * math.pi / NFFT)
    factor = 1.0 / math.sqrt(NFFT)
    rows = np.concatenate([np.cos(phase) * factor, -np.sin(phase) * factor], axis=0)
    return rows.astype(np.float32).astype(ml_dtypes.bfloat16)


def channelize_kernel(v_ref, halo_ref, taps_ref, table_ref, out_ref, past_ref, filt_ref, spec_ref):
    inputs = v_ref.shape[0]
    spectra = v_ref.shape[1] // NFFT

    @pl.when(pl.program_id(0) == 0)
    def _():
        past_ref[...] = halo_ref[...]

    for lane in range(0, NFFT, LANES):
        taps = [
            jnp.broadcast_to(taps_ref[t : t + 1, lane : lane + LANES], (inputs, LANES))
            for t in range(TAPS)
        ]
        past = tuple(
            past_ref[:, t * NFFT + lane : t * NFFT + lane + LANES].astype(jnp.float32)
            for t in range(TAPS - 1)
        )

        def step(g, past, lane=lane, taps=taps):
            window = list(past)
            rows = []
            for s in range(GROUP):
                at = pl.multiple_of((g * GROUP + s) * NFFT + lane, LANES)
                window.append(v_ref[:, pl.ds(at, LANES)].astype(jnp.float32))
                total = taps[0] * window[0]
                for t in range(1, TAPS):
                    total = total + taps[t] * window[t]
                rows.append(total.astype(jnp.bfloat16))
                window = window[1:]
            block = jnp.swapaxes(jnp.stack(rows, axis=0), 0, 1)
            first = pl.multiple_of(g * GROUP, GROUP)
            filt_ref[:, pl.ds(first, GROUP), lane : lane + LANES] = block
            return tuple(window)

        lax.fori_loop(0, spectra // GROUP, step, past)

    past_ref[...] = v_ref[:, (spectra - (TAPS - 1)) * NFFT :]

    pair = 2

    @pl.loop(0, inputs // pair)
    def _(p):
        rhs = filt_ref[pl.ds(p * pair, pair)].reshape(pair * spectra, NFFT)
        result = lax.dot_general(
            table_ref[...], rhs, (((1,), (1,)), ((), ())), preferred_element_type=jnp.float32
        ).astype(jnp.bfloat16)
        for i in range(pair):
            spec_ref[p * pair + i] = result[:, i * spectra : (i + 1) * spectra]

    @pl.loop(0, CHANNELS // GROUP)
    def _(g):
        first = pl.multiple_of(g * GROUP, GROUP)
        for r in range(2):
            block = spec_ref[:, pl.ds(r * CHANNELS + first, GROUP), :]
            out_ref[pl.ds(first, GROUP), :, r * spectra : (r + 1) * spectra] = jnp.swapaxes(
                block, 0, 1
            )


def channelize(voltages, halo, taps):
    inputs, samples = voltages.shape
    chunk = LANES
    spectra = samples // NFFT
    steps = spectra // chunk
    return pl.pallas_call(
        channelize_kernel,
        name="channelize",
        grid=(steps,),
        out_shape=jax.ShapeDtypeStruct((CHANNELS, inputs, 2 * spectra), jnp.bfloat16),
        in_specs=[
            pl.BlockSpec((inputs, chunk * NFFT), lambda c: (0, c)),
            pl.BlockSpec(halo.shape, lambda c: (0, 0)),
            pl.BlockSpec(taps.shape, lambda c: (0, 0)),
            pl.BlockSpec((NFFT, NFFT), lambda c: (0, 0)),
        ],
        out_specs=pl.BlockSpec((CHANNELS, inputs, 2 * chunk), lambda c: (0, 0, c)),
        scratch_shapes=[
            pltpu.VMEM(halo.shape, jnp.bfloat16),
            pltpu.VMEM((inputs, chunk, NFFT), jnp.bfloat16),
            pltpu.VMEM((inputs, NFFT, chunk), jnp.bfloat16),
        ],
        compiler_params=pltpu.CompilerParams(vmem_limit_bytes=40 << 20),
        cost_estimate=pl.CostEstimate(
            flops=2 * inputs * samples * NFFT, bytes_accessed=4 * inputs * samples, transcendentals=0
        ),
    )(voltages, halo, taps, jnp.asarray(fourier_rows()))


def correlate_kernel(x_ref, out_ref):
    width = x_ref.shape[-1]
    x = x_ref[...].reshape(-1, width)
    parts = []
    for at in range(0, width, 2 * LANES):
        parts.append(x[:, at + LANES : at + 2 * LANES])
        parts.append(-x[:, at : at + LANES])
    turned = jnp.concatenate(parts, axis=1)
    dims = (((1,), (1,)), ((), ()))
    scale = 2.0 / width
    real = lax.dot_general(x, x, dims, preferred_element_type=jnp.float32)
    out_ref[0, 0, 0] = real * scale
    imag = lax.dot_general(turned, x, dims, preferred_element_type=jnp.float32)
    out_ref[0, 0, 1] = imag * scale


def correlate(received):
    dumps, sources, channels, inputs, width = received.shape
    count = sources * inputs
    return pl.pallas_call(
        correlate_kernel,
        name="correlate",
        grid=(dumps, channels),
        out_shape=jax.ShapeDtypeStruct((dumps, channels, 2, count, count), jnp.float32),
        in_specs=[pl.BlockSpec((1, sources, 1, inputs, width), lambda d, c: (d, 0, c, 0, 0))],
        out_specs=pl.BlockSpec((1, 1, 2, count, count), lambda d, c: (d, c, 0, 0, 0)),
        compiler_params=pltpu.CompilerParams(vmem_limit_bytes=40 << 20),
        cost_estimate=pl.CostEstimate(
            flops=4 * dumps * channels * count * count * width,
            bytes_accessed=8 * dumps * channels * count * count,
            transcendentals=0,
        ),
    )(received)


def on_device(voltages, filter_taps):
    dumps = lax.axis_size("tm")
    sources = lax.axis_size("inputs")
    tail = voltages[:, voltages.shape[1] - (TAPS - 1) * NFFT :]
    halo = lax.ppermute(tail, "tm", [(i, i + 1) for i in range(dumps - 1)])
    spectra = channelize(voltages, halo, filter_taps)
    moved = lax.all_to_all(spectra, ("tm", "inputs"), split_axis=0, concat_axis=0, tiled=True)
    received = moved.reshape(
        dumps, sources, moved.shape[0] // (dumps * sources), moved.shape[1], moved.shape[2]
    )
    return correlate(received)


def solution(mesh):
    in_specs = (P("inputs", "tm"), P())
    out_specs = P(None, ("tm", "inputs"), None, None, None)
    return jax.shard_map(
        on_device, mesh=mesh, in_specs=in_specs, out_specs=out_specs, check_vma=False
    )
```

```python
import math

import jax
import jax.numpy as jnp
import ml_dtypes
import numpy as np
from jax import lax
from jax.experimental import pallas as pl
from jax.experimental.pallas import tpu as pltpu
from jax.sharding import PartitionSpec as P

NFFT = 512
TAPS = 4
CHANNELS = NFFT // 2
LANES = 128
GROUP = 16
PAIR = 2
UNROLL = 2
ROWS_BY_ROWS = (((1,), (1,)), ((), ()))


def fourier_rows():
    n = np.arange(NFFT)
    k = np.arange(CHANNELS)
    phase = (k[:, None] * n[None, :] % NFFT) * (2.0 * math.pi / NFFT)
    factor = 1.0 / math.sqrt(NFFT)
    rows = np.concatenate([np.cos(phase) * factor, -np.sin(phase) * factor], axis=0)
    return rows.astype(np.float32).astype(ml_dtypes.bfloat16)


def filter_group(samples_ref, first, past, taps_ref, store):
    inputs = samples_ref.shape[0]
    for lane in range(0, NFFT, LANES):
        taps = [
            jnp.broadcast_to(taps_ref[t : t + 1, lane : lane + LANES], (inputs, LANES))
            for t in range(TAPS)
        ]
        window = [past(t, lane).astype(jnp.float32) for t in range(TAPS - 1)]
        rows = []
        for s in range(GROUP):
            at = pl.multiple_of((first + s) * NFFT + lane, LANES)
            window.append(samples_ref[:, pl.ds(at, LANES)].astype(jnp.float32))
            total = taps[0] * window[0]
            for t in range(1, TAPS):
                total = total + taps[t] * window[t]
            rows.append(total.astype(jnp.bfloat16))
            window = window[1:]
        store(lane, jnp.swapaxes(jnp.stack(rows, axis=0), 0, 1))


def transform(table_ref, rows, out_ref, p):
    spectra = rows.shape[1]
    result = lax.dot_general(
        table_ref[...],
        rows.reshape(PAIR * spectra, NFFT),
        ROWS_BY_ROWS,
        preferred_element_type=jnp.float32,
    ).astype(jnp.bfloat16)
    for i in range(PAIR):
        out_ref[p * PAIR + i] = result[:, i * spectra : (i + 1) * spectra]


def swap_group(spec_ref, out_ref, g, lane):
    first = pl.multiple_of(g * GROUP, GROUP)
    for r in range(2):
        block = spec_ref[:, pl.ds(r * CHANNELS + first, GROUP), :]
        at = lane + r * LANES
        out_ref[pl.ds(first, GROUP), :, at : at + LANES] = jnp.swapaxes(block, 0, 1)


def loop(steps, body):
    @pl.loop(0, steps // UNROLL)
    def _(i):
        for u in range(UNROLL):
            body(i * UNROLL + u)


def early_kernel(
    v_hbm, taps_hbm, table_hbm, spec_ref, filt_ref, head_ref, v_ref, taps_ref, table_ref, late_ref, sems
):
    inputs = v_ref.shape[0]
    groups = v_ref.shape[1] // (GROUP * NFFT)
    half = groups // 2
    order = [(half - 1, 2)] + [(g, min(2, groups - g)) for g in range(half + 1, groups, 2)]
    order += [(g, min(2, half - 1 - g)) for g in range(0, half - 1, 2)]
    copies = [
        pltpu.make_async_copy(taps_hbm, taps_ref, sems.at[0]),
        pltpu.make_async_copy(table_hbm, table_ref, sems.at[1]),
    ]
    copies[0].start()
    parts = []
    for i, (g, count) in enumerate(order):
        span = pl.ds(g * GROUP * NFFT, count * GROUP * NFFT)
        parts.append(pltpu.make_async_copy(v_hbm.at[:, span], v_ref.at[:, span], sems.at[2 + i]))
        parts[-1].start()
        if i == 0:
            copies[1].start()
    copies[0].wait()

    def run(g, target, at):
        first = g * GROUP

        def past(t, lane):
            start = pl.multiple_of((first - (TAPS - 1) + t) * NFFT + lane, LANES)
            return v_ref[:, pl.ds(start, LANES)]

        def store(lane, block):
            target[:, pl.ds(pl.multiple_of(at * GROUP, GROUP), GROUP), lane : lane + LANES] = block

        filter_group(v_ref, first, past, taps_ref, store)

    late = groups - half
    for i, (g, count) in enumerate(order):
        if g < half - 1:
            break
        parts[i].wait()
        for q in range(count):
            if g + q >= half:
                run(g + q, late_ref, g + q - half)
    for part in parts[i:]:
        part.wait()
    copies[1].wait()
    head_ref[...] = v_ref[:, : GROUP * NFFT]

    def both(p):
        rows = late_ref[pl.ds(p * PAIR, PAIR)]
        transform(table_ref, rows, spec_ref, p)
        run(jnp.maximum(p, 1), filt_ref, jnp.maximum(p, 1))

    loop(inputs // PAIR, both)


def early(voltages, taps, table):
    inputs, samples = voltages.shape
    spectra = samples // NFFT
    any_spec = pl.BlockSpec(memory_space=pltpu.HBM)
    vmem_spec = pl.BlockSpec(memory_space=pltpu.VMEM)
    return pl.pallas_call(
        early_kernel,
        name="early",
        out_shape=(
            jax.ShapeDtypeStruct((inputs, NFFT, spectra // 2), jnp.bfloat16),
            jax.ShapeDtypeStruct((inputs, spectra // 2, NFFT), jnp.bfloat16),
            jax.ShapeDtypeStruct((inputs, GROUP * NFFT), jnp.bfloat16),
        ),
        in_specs=[any_spec] * 3,
        out_specs=(vmem_spec,) * 3,
        scratch_shapes=[
            pltpu.VMEM(voltages.shape, jnp.bfloat16),
            pltpu.VMEM(taps.shape, jnp.float32),
            pltpu.VMEM(table.shape, jnp.bfloat16),
            pltpu.VMEM((inputs, spectra // 2, NFFT), jnp.bfloat16),
            pltpu.SemaphoreType.DMA((2 + spectra // GROUP,)),
        ],
        compiler_params=pltpu.CompilerParams(vmem_limit_bytes=24 << 20),
        cost_estimate=pl.CostEstimate(
            flops=inputs * samples * NFFT, bytes_accessed=2 * inputs * samples, transcendentals=0
        ),
    )(voltages, taps, table)


def late_kernel(halo_ref, head_ref, taps_ref, table_ref, filt_ref, early_ref, out_ref, first_ref, spec_ref):
    inputs = head_ref.shape[0]

    def past(t, lane):
        return halo_ref[:, t * NFFT + lane : t * NFFT + lane + LANES]

    def store(lane, block):
        first_ref[:, :, lane : lane + LANES] = block

    filter_group(head_ref, 0, past, taps_ref, store)
    pairs = inputs // PAIR
    groups = CHANNELS // GROUP

    def both(p):
        pair = pl.ds(p * PAIR, PAIR)
        rows = jnp.concatenate([first_ref[pair], filt_ref[pair, GROUP:, :]], axis=1)
        transform(table_ref, rows, spec_ref, p)
        for q in range(groups // pairs):
            swap_group(early_ref, out_ref, p * (groups // pairs) + q, 2 * LANES)

    loop(pairs, both)

    def rest(g):
        swap_group(spec_ref, out_ref, g, 0)

    loop(groups, rest)


def late(halo, head, taps, table, filt, spec):
    inputs, spectra, _ = filt.shape
    vmem_spec = pl.BlockSpec(memory_space=pltpu.VMEM)
    return pl.pallas_call(
        late_kernel,
        name="late",
        out_shape=jax.ShapeDtypeStruct((CHANNELS, inputs, 4 * spectra), jnp.bfloat16),
        in_specs=[vmem_spec] * 6,
        out_specs=vmem_spec,
        scratch_shapes=[
            pltpu.VMEM((inputs, GROUP, NFFT), jnp.bfloat16),
            pltpu.VMEM((inputs, NFFT, spectra), jnp.bfloat16),
        ],
        compiler_params=pltpu.CompilerParams(vmem_limit_bytes=20 << 20),
        cost_estimate=pl.CostEstimate(
            flops=2 * inputs * spectra * NFFT * NFFT,
            bytes_accessed=4 * inputs * spectra * NFFT,
            transcendentals=0,
        ),
    )(halo, head, taps, table, filt, spec)


def correlate_kernel(x_ref, out_hbm, out_ref, sems):
    dumps, sources, channels, inputs, width = x_ref.shape
    scale = 2.0 / width
    copies = []

    def send(step, part):
        target = out_hbm.at[step // channels, step % channels, part]
        copies.append(pltpu.make_async_copy(out_ref.at[step, part], target, sems.at[step, part]))
        copies[-1].start()

    for step in range(dumps * channels):
        x = x_ref[step // channels, :, step % channels].reshape(sources * inputs, width)
        real = lax.dot_general(x, x, ROWS_BY_ROWS, preferred_element_type=jnp.float32)
        out_ref[step, 0] = real * scale
        send(step, 0)
        turned = []
        for at in range(0, width, 2 * LANES):
            turned += [x[:, at + LANES : at + 2 * LANES], -x[:, at : at + LANES]]
        imag = lax.dot_general(
            jnp.concatenate(turned, axis=1), x, ROWS_BY_ROWS, preferred_element_type=jnp.float32
        )
        out_ref[step, 1] = imag * scale
        send(step, 1)
    for copy in copies:
        copy.wait()


def correlate(received):
    dumps, sources, channels, inputs, width = received.shape
    count = sources * inputs
    steps = dumps * channels
    return pl.pallas_call(
        correlate_kernel,
        name="correlate",
        out_shape=jax.ShapeDtypeStruct((dumps, channels, 2, count, count), jnp.float32),
        in_specs=[pl.BlockSpec(memory_space=pltpu.VMEM)],
        out_specs=pl.BlockSpec(memory_space=pltpu.HBM),
        scratch_shapes=[
            pltpu.VMEM((steps, 2, count, count), jnp.float32),
            pltpu.SemaphoreType.DMA((steps, 2)),
        ],
        compiler_params=pltpu.CompilerParams(vmem_limit_bytes=30 << 20),
        cost_estimate=pl.CostEstimate(
            flops=4 * steps * count * count * width,
            bytes_accessed=8 * steps * count * count,
            transcendentals=0,
        ),
    )(received)


def on_device(voltages, filter_taps):
    dumps = lax.axis_size("tm")
    sources = lax.axis_size("inputs")
    table = jnp.asarray(fourier_rows())
    tail = voltages[:, voltages.shape[1] - (TAPS - 1) * NFFT :]
    halo = lax.ppermute(tail, "tm", [(i, i + 1) for i in range(dumps - 1)])
    spec, filt, head = early(
        pltpu.with_memory_space_constraint(voltages, pltpu.HBM),
        pltpu.with_memory_space_constraint(filter_taps, pltpu.HBM),
        pltpu.with_memory_space_constraint(table, pltpu.HBM),
    )
    spectra = late(halo, head, filter_taps, table, filt, spec)
    moved = lax.all_to_all(spectra, ("tm", "inputs"), split_axis=0, concat_axis=0, tiled=True)
    received = moved.reshape(
        dumps, sources, moved.shape[0] // (dumps * sources), moved.shape[1], moved.shape[2]
    )
    return correlate(received)


def solution(mesh):
    in_specs = (P("inputs", "tm"), P())
    out_specs = P(None, ("tm", "inputs"), None, None, None)
    return jax.shard_map(
        on_device, mesh=mesh, in_specs=in_specs, out_specs=out_specs, check_vma=False
    )
```

```python
import math

import jax
import jax.numpy as jnp
import ml_dtypes
import numpy as np
from jax import lax
from jax.experimental import pallas as pl
from jax.experimental.pallas import tpu as pltpu
from jax.sharding import PartitionSpec as P

NFFT = 512
TAPS = 4
CHANNELS = NFFT // 2
LANES = 128
GROUP = 16
PAIR = 2
FIRST_UNROLL = 2
BOTH_UNROLL = 2
LATE_UNROLL = 8
REST_UNROLL = 4
ROWS_BY_ROWS = (((1,), (1,)), ((), ()))


def fourier_rows():
    n = np.arange(NFFT)
    k = np.arange(CHANNELS)
    phase = (k[:, None] * n[None, :] % NFFT) * (2.0 * math.pi / NFFT)
    factor = 1.0 / math.sqrt(NFFT)
    rows = np.concatenate([np.cos(phase) * factor, -np.sin(phase) * factor], axis=0)
    return rows.astype(np.float32).astype(ml_dtypes.bfloat16)


def filter_group(samples_ref, first, past, taps_ref, store):
    inputs = samples_ref.shape[0]
    for lane in range(0, NFFT, LANES):
        taps = [
            jnp.broadcast_to(taps_ref[t : t + 1, lane : lane + LANES], (inputs, LANES))
            for t in range(TAPS)
        ]
        window = [past(t, lane).astype(jnp.float32) for t in range(TAPS - 1)]
        rows = []
        for s in range(GROUP):
            at = pl.multiple_of((first + s) * NFFT + lane, LANES)
            window.append(samples_ref[:, pl.ds(at, LANES)].astype(jnp.float32))
            total = taps[0] * window[0]
            for t in range(1, TAPS):
                total = total + taps[t] * window[t]
            rows.append(total.astype(jnp.bfloat16))
            window = window[1:]
        store(lane, jnp.swapaxes(jnp.stack(rows, axis=0), 0, 1))


def transform(table_ref, rows, out_ref, p):
    spectra = rows.shape[1]
    result = lax.dot_general(
        table_ref[...],
        rows.reshape(PAIR * spectra, NFFT),
        ROWS_BY_ROWS,
        preferred_element_type=jnp.float32,
    ).astype(jnp.bfloat16)
    for i in range(PAIR):
        out_ref[p * PAIR + i] = result[:, i * spectra : (i + 1) * spectra]


def swap_group(spec_ref, out_ref, g, lane):
    first = pl.multiple_of(g * GROUP, GROUP)
    for r in range(2):
        block = spec_ref[:, pl.ds(r * CHANNELS + first, GROUP), :]
        at = lane + r * LANES
        out_ref[pl.ds(first, GROUP), :, at : at + LANES] = jnp.swapaxes(block, 0, 1)


def loop(steps, body, unroll):
    if unroll == steps:
        for i in range(steps):
            body(i)
        return

    @pl.loop(0, steps // unroll)
    def _(i):
        for u in range(unroll):
            body(i * unroll + u)


def early_kernel(
    v_hbm, taps_hbm, table_hbm, spec_ref, filt_ref, head_ref, v_ref, taps_ref, table_ref, late_ref, sems
):
    inputs = v_ref.shape[0]
    groups = v_ref.shape[1] // (GROUP * NFFT)
    half = groups // 2

    def part(g):
        span = pl.ds(pl.multiple_of(g * GROUP * NFFT, LANES), GROUP * NFFT)
        return pltpu.make_async_copy(v_hbm.at[:, span], v_ref.at[:, span], sems.at[g])

    taps_copy = pltpu.make_async_copy(taps_hbm, taps_ref, sems.at[groups])
    table_copy = pltpu.make_async_copy(table_hbm, table_ref, sems.at[groups + 1])
    taps_copy.start()
    for g in range(half - 1, groups):
        part(g).start()
    table_copy.start()
    for g in range(half - 1):
        part(g).start()

    def run(g, target, at):
        first = g * GROUP

        def past(t, lane):
            start = pl.multiple_of((first - (TAPS - 1) + t) * NFFT + lane, LANES)
            return v_ref[:, pl.ds(start, LANES)]

        def store(lane, block):
            target[:, pl.ds(pl.multiple_of(at * GROUP, GROUP), GROUP), lane : lane + LANES] = block

        filter_group(v_ref, first, past, taps_ref, store)

    taps_copy.wait()
    part(half - 1).wait()

    def second_half(i):
        part(half + i).wait()
        run(half + i, late_ref, i)

    loop(groups - half, second_half, FIRST_UNROLL)
    table_copy.wait()
    for g in range(half - 1):
        part(g).wait()
    head_ref[...] = v_ref[:, : GROUP * NFFT]

    def both(p):
        rows = late_ref[pl.ds(p * PAIR, PAIR)]
        transform(table_ref, rows, spec_ref, p)
        run(jnp.maximum(p, 1), filt_ref, jnp.maximum(p, 1))

    loop(inputs // PAIR, both, BOTH_UNROLL)


def early(voltages, taps, table):
    inputs, samples = voltages.shape
    spectra = samples // NFFT
    any_spec = pl.BlockSpec(memory_space=pltpu.HBM)
    vmem_spec = pl.BlockSpec(memory_space=pltpu.VMEM)
    return pl.pallas_call(
        early_kernel,
        name="early",
        out_shape=(
            jax.ShapeDtypeStruct((inputs, NFFT, spectra // 2), jnp.bfloat16),
            jax.ShapeDtypeStruct((inputs, spectra // 2, NFFT), jnp.bfloat16),
            jax.ShapeDtypeStruct((inputs, GROUP * NFFT), jnp.bfloat16),
        ),
        in_specs=[any_spec] * 3,
        out_specs=(vmem_spec,) * 3,
        scratch_shapes=[
            pltpu.VMEM(voltages.shape, jnp.bfloat16),
            pltpu.VMEM(taps.shape, jnp.float32),
            pltpu.VMEM(table.shape, jnp.bfloat16),
            pltpu.VMEM((inputs, spectra // 2, NFFT), jnp.bfloat16),
            pltpu.SemaphoreType.DMA((2 + spectra // GROUP,)),
        ],
        compiler_params=pltpu.CompilerParams(vmem_limit_bytes=24 << 20),
        cost_estimate=pl.CostEstimate(
            flops=inputs * samples * NFFT, bytes_accessed=2 * inputs * samples, transcendentals=0
        ),
    )(voltages, taps, table)


def late_kernel(halo_ref, head_ref, taps_ref, table_ref, filt_ref, early_ref, out_ref, first_ref, spec_ref):
    inputs = head_ref.shape[0]
    started = lax.axis_index("tm") > 0

    def past(t, lane):
        block = halo_ref[:, t * NFFT + lane : t * NFFT + lane + LANES].astype(jnp.float32)
        return jnp.where(started, block, 0.0)

    def store(lane, block):
        first_ref[:, :, lane : lane + LANES] = block

    filter_group(head_ref, 0, past, taps_ref, store)
    pairs = inputs // PAIR
    groups = CHANNELS // GROUP

    def both(p):
        pair = pl.ds(p * PAIR, PAIR)
        rows = jnp.concatenate([first_ref[pair], filt_ref[pair, GROUP:, :]], axis=1)
        transform(table_ref, rows, spec_ref, p)
        for q in range(groups // pairs):
            swap_group(early_ref, out_ref, p * (groups // pairs) + q, 2 * LANES)

    loop(pairs, both, LATE_UNROLL)

    def rest(g):
        swap_group(spec_ref, out_ref, g, 0)

    loop(groups, rest, REST_UNROLL)


def late(halo, head, taps, table, filt, spec):
    inputs, spectra, _ = filt.shape
    vmem_spec = pl.BlockSpec(memory_space=pltpu.VMEM)
    return pl.pallas_call(
        late_kernel,
        name="late",
        out_shape=jax.ShapeDtypeStruct((CHANNELS, inputs, 4 * spectra), jnp.bfloat16),
        in_specs=[vmem_spec] * 6,
        out_specs=vmem_spec,
        scratch_shapes=[
            pltpu.VMEM((inputs, GROUP, NFFT), jnp.bfloat16),
            pltpu.VMEM((inputs, NFFT, spectra), jnp.bfloat16),
        ],
        compiler_params=pltpu.CompilerParams(vmem_limit_bytes=20 << 20),
        cost_estimate=pl.CostEstimate(
            flops=2 * inputs * spectra * NFFT * NFFT,
            bytes_accessed=4 * inputs * spectra * NFFT,
            transcendentals=0,
        ),
    )(halo, head, taps, table, filt, spec)


def correlate_kernel(x_ref, out_hbm, out_ref, sems):
    dumps, sources, channels, inputs, width = x_ref.shape
    scale = 2.0 / width
    copies = []

    def send(step, part):
        target = out_hbm.at[step // channels, step % channels, part]
        copies.append(pltpu.make_async_copy(out_ref.at[step, part], target, sems.at[step, part]))
        copies[-1].start()

    for step in range(dumps * channels):
        x = x_ref[step // channels, :, step % channels].reshape(sources * inputs, width)
        real = lax.dot_general(x, x, ROWS_BY_ROWS, preferred_element_type=jnp.float32)
        out_ref[step, 0] = real * scale
        send(step, 0)
        turned = []
        for at in range(0, width, 2 * LANES):
            turned += [x[:, at + LANES : at + 2 * LANES], -x[:, at : at + LANES]]
        imag = lax.dot_general(
            jnp.concatenate(turned, axis=1), x, ROWS_BY_ROWS, preferred_element_type=jnp.float32
        )
        out_ref[step, 1] = imag * scale
        send(step, 1)
    for copy in copies:
        copy.wait()


def correlate(received):
    dumps, sources, channels, inputs, width = received.shape
    count = sources * inputs
    steps = dumps * channels
    return pl.pallas_call(
        correlate_kernel,
        name="correlate",
        out_shape=jax.ShapeDtypeStruct((dumps, channels, 2, count, count), jnp.float32),
        in_specs=[pl.BlockSpec(memory_space=pltpu.VMEM)],
        out_specs=pl.BlockSpec(memory_space=pltpu.HBM),
        scratch_shapes=[
            pltpu.VMEM((steps, 2, count, count), jnp.float32),
            pltpu.SemaphoreType.DMA((steps, 2)),
        ],
        compiler_params=pltpu.CompilerParams(vmem_limit_bytes=30 << 20),
        cost_estimate=pl.CostEstimate(
            flops=4 * steps * count * count * width,
            bytes_accessed=8 * steps * count * count,
            transcendentals=0,
        ),
    )(received)


def on_device(voltages, filter_taps):
    dumps = lax.axis_size("tm")
    sources = lax.axis_size("inputs")
    table = jnp.asarray(fourier_rows())
    tail = voltages[:, voltages.shape[1] - (TAPS - 1) * NFFT :]
    halo = lax.ppermute(tail, "tm", [(i, (i + 1) % dumps) for i in range(dumps)])
    spec, filt, head = early(
        pltpu.with_memory_space_constraint(voltages, pltpu.HBM),
        pltpu.with_memory_space_constraint(filter_taps, pltpu.HBM),
        pltpu.with_memory_space_constraint(table, pltpu.HBM),
    )
    spectra = late(halo, head, filter_taps, table, filt, spec)
    moved = lax.all_to_all(spectra, ("tm", "inputs"), split_axis=0, concat_axis=0, tiled=True)
    received = moved.reshape(
        dumps, sources, moved.shape[0] // (dumps * sources), moved.shape[1], moved.shape[2]
    )
    return correlate(received)


def solution(mesh):
    in_specs = (P("inputs", "tm"), P())
    out_specs = P(None, ("tm", "inputs"), None, None, None)
    return jax.shard_map(
        on_device, mesh=mesh, in_specs=in_specs, out_specs=out_specs, check_vma=False
    )
```

```python
import math

import jax
import jax.numpy as jnp
import ml_dtypes
import numpy as np
from jax import lax
from jax.experimental import pallas as pl
from jax.experimental.pallas import tpu as pltpu
from jax.sharding import PartitionSpec as P

NFFT = 512
TAPS = 4
CHANNELS = NFFT // 2
LANES = 128
GROUP = 16
PAIR = 2
FIRST_UNROLL = 2
BOTH_UNROLL = 2
LATE_UNROLL = 8
REST_UNROLL = 4
ROWS_BY_ROWS = (((1,), (1,)), ((), ()))


def fourier_rows(owners, groups):
    n = np.arange(NFFT)
    k = np.arange(CHANNELS).reshape(groups, owners, -1).transpose(1, 0, 2).reshape(-1)
    phase = (k[:, None] * n[None, :] % NFFT) * (2.0 * math.pi / NFFT)
    factor = 1.0 / math.sqrt(NFFT)
    rows = np.concatenate([np.cos(phase) * factor, -np.sin(phase) * factor], axis=0)
    return rows.astype(np.float32).astype(ml_dtypes.bfloat16)


def filter_group(samples_ref, first, past, taps_ref, store):
    inputs = samples_ref.shape[0]
    for lane in range(0, NFFT, LANES):
        taps = [
            jnp.broadcast_to(taps_ref[t : t + 1, lane : lane + LANES], (inputs, LANES))
            for t in range(TAPS)
        ]
        window = [past(t, lane).astype(jnp.float32) for t in range(TAPS - 1)]
        rows = []
        for s in range(GROUP):
            at = pl.multiple_of((first + s) * NFFT + lane, LANES)
            window.append(samples_ref[:, pl.ds(at, LANES)].astype(jnp.float32))
            total = taps[0] * window[0]
            for t in range(1, TAPS):
                total = total + taps[t] * window[t]
            rows.append(total.astype(jnp.bfloat16))
            window = window[1:]
        store(lane, jnp.swapaxes(jnp.stack(rows, axis=0), 0, 1))


def transform(table_ref, rows, out_ref, p):
    spectra = rows.shape[1]
    result = lax.dot_general(
        table_ref[...],
        rows.reshape(PAIR * spectra, NFFT),
        ROWS_BY_ROWS,
        preferred_element_type=jnp.float32,
    ).astype(jnp.bfloat16)
    for i in range(PAIR):
        out_ref[p * PAIR + i] = result[:, i * spectra : (i + 1) * spectra]


def swap_group(spec_ref, out_ref, g, lane):
    first = pl.multiple_of(g * GROUP, GROUP)
    for r in range(2):
        block = spec_ref[:, pl.ds(r * CHANNELS + first, GROUP), :]
        at = lane + r * LANES
        out_ref[pl.ds(first, GROUP), :, at : at + LANES] = jnp.swapaxes(block, 0, 1)


def loop(steps, body, unroll):
    if unroll == steps:
        for i in range(steps):
            body(i)
        return

    @pl.loop(0, steps // unroll)
    def _(i):
        for u in range(unroll):
            body(i * unroll + u)


def early_kernel(
    v_hbm, taps_hbm, table_hbm, spec_ref, filt_ref, head_ref, v_ref, taps_ref, table_ref, late_ref, sems
):
    inputs = v_ref.shape[0]
    groups = v_ref.shape[1] // (GROUP * NFFT)
    half = groups // 2

    def part(g):
        span = pl.ds(pl.multiple_of(g * GROUP * NFFT, LANES), GROUP * NFFT)
        return pltpu.make_async_copy(v_hbm.at[:, span], v_ref.at[:, span], sems.at[g])

    taps_copy = pltpu.make_async_copy(taps_hbm, taps_ref, sems.at[groups])
    table_copy = pltpu.make_async_copy(table_hbm, table_ref, sems.at[groups + 1])
    taps_copy.start()
    for g in range(half - 1, groups):
        part(g).start()
    table_copy.start()
    for g in range(half - 1):
        part(g).start()

    def run(g, target, at):
        first = g * GROUP

        def past(t, lane):
            start = pl.multiple_of((first - (TAPS - 1) + t) * NFFT + lane, LANES)
            return v_ref[:, pl.ds(start, LANES)]

        def store(lane, block):
            target[:, pl.ds(pl.multiple_of(at * GROUP, GROUP), GROUP), lane : lane + LANES] = block

        filter_group(v_ref, first, past, taps_ref, store)

    taps_copy.wait()
    part(half - 1).wait()

    def second_half(i):
        part(half + i).wait()
        run(half + i, late_ref, i)

    loop(groups - half, second_half, FIRST_UNROLL)
    table_copy.wait()
    for g in range(half - 1):
        part(g).wait()
    head_ref[...] = v_ref[:, : GROUP * NFFT]

    def both(p):
        rows = late_ref[pl.ds(p * PAIR, PAIR)]
        transform(table_ref, rows, spec_ref, p)
        run(jnp.maximum(p, 1), filt_ref, jnp.maximum(p, 1))

    loop(inputs // PAIR, both, BOTH_UNROLL)


def early(voltages, taps, table):
    inputs, samples = voltages.shape
    spectra = samples // NFFT
    any_spec = pl.BlockSpec(memory_space=pltpu.HBM)
    vmem_spec = pl.BlockSpec(memory_space=pltpu.VMEM)
    return pl.pallas_call(
        early_kernel,
        name="early",
        out_shape=(
            jax.ShapeDtypeStruct((inputs, NFFT, spectra // 2), jnp.bfloat16),
            jax.ShapeDtypeStruct((inputs, spectra // 2, NFFT), jnp.bfloat16),
            jax.ShapeDtypeStruct((inputs, GROUP * NFFT), jnp.bfloat16),
        ),
        in_specs=[any_spec] * 3,
        out_specs=(vmem_spec,) * 3,
        scratch_shapes=[
            pltpu.VMEM(voltages.shape, jnp.bfloat16),
            pltpu.VMEM(taps.shape, jnp.float32),
            pltpu.VMEM(table.shape, jnp.bfloat16),
            pltpu.VMEM((inputs, spectra // 2, NFFT), jnp.bfloat16),
            pltpu.SemaphoreType.DMA((2 + spectra // GROUP,)),
        ],
        compiler_params=pltpu.CompilerParams(vmem_limit_bytes=24 << 20),
        cost_estimate=pl.CostEstimate(
            flops=inputs * samples * NFFT, bytes_accessed=2 * inputs * samples, transcendentals=0
        ),
    )(voltages, taps, table)


def late_kernel(halo_ref, head_ref, taps_ref, table_ref, filt_ref, early_ref, out_ref, first_ref, spec_ref):
    inputs = head_ref.shape[0]
    started = lax.axis_index("tm") > 0

    def past(t, lane):
        block = halo_ref[:, t * NFFT + lane : t * NFFT + lane + LANES].astype(jnp.float32)
        return jnp.where(started, block, 0.0)

    def store(lane, block):
        first_ref[:, :, lane : lane + LANES] = block

    filter_group(head_ref, 0, past, taps_ref, store)
    pairs = inputs // PAIR
    groups = CHANNELS // GROUP

    def both(p):
        pair = pl.ds(p * PAIR, PAIR)
        rows = jnp.concatenate([first_ref[pair], filt_ref[pair, GROUP:, :]], axis=1)
        transform(table_ref, rows, spec_ref, p)
        for q in range(groups // pairs):
            swap_group(early_ref, out_ref, p * (groups // pairs) + q, 2 * LANES)

    loop(pairs, both, LATE_UNROLL)

    def rest(g):
        swap_group(spec_ref, out_ref, g, 0)

    loop(groups, rest, REST_UNROLL)


def late(halo, head, taps, table, filt, spec):
    inputs, spectra, _ = filt.shape
    vmem_spec = pl.BlockSpec(memory_space=pltpu.VMEM)
    return pl.pallas_call(
        late_kernel,
        name="late",
        out_shape=jax.ShapeDtypeStruct((CHANNELS, inputs, 4 * spectra), jnp.bfloat16),
        in_specs=[vmem_spec] * 6,
        out_specs=vmem_spec,
        scratch_shapes=[
            pltpu.VMEM((inputs, GROUP, NFFT), jnp.bfloat16),
            pltpu.VMEM((inputs, NFFT, spectra), jnp.bfloat16),
        ],
        compiler_params=pltpu.CompilerParams(vmem_limit_bytes=20 << 20),
        cost_estimate=pl.CostEstimate(
            flops=2 * inputs * spectra * NFFT * NFFT,
            bytes_accessed=4 * inputs * spectra * NFFT,
            transcendentals=0,
        ),
    )(halo, head, taps, table, filt, spec)


def correlate_kernel(x_ref, out_hbm, out_ref, sems):
    sources, dumps, channels, inputs, width = x_ref.shape
    scale = 2.0 / width
    copies = []

    def send(step, part):
        target = out_hbm.at[step // channels, step % channels, part]
        copies.append(pltpu.make_async_copy(out_ref.at[step, part], target, sems.at[step, part]))
        copies[-1].start()

    for step in range(dumps * channels):
        x = x_ref[:, step // channels, step % channels].reshape(sources * inputs, width)
        real = lax.dot_general(x, x, ROWS_BY_ROWS, preferred_element_type=jnp.float32)
        out_ref[step, 0] = real * scale
        send(step, 0)
        turned = []
        for at in range(0, width, 2 * LANES):
            turned += [x[:, at + LANES : at + 2 * LANES], -x[:, at : at + LANES]]
        imag = lax.dot_general(
            jnp.concatenate(turned, axis=1), x, ROWS_BY_ROWS, preferred_element_type=jnp.float32
        )
        out_ref[step, 1] = imag * scale
        send(step, 1)
    for copy in copies:
        copy.wait()


def correlate(received):
    sources, dumps, channels, inputs, width = received.shape
    count = sources * inputs
    steps = dumps * channels
    return pl.pallas_call(
        correlate_kernel,
        name="correlate",
        out_shape=jax.ShapeDtypeStruct((dumps, channels, 2, count, count), jnp.float32),
        in_specs=[pl.BlockSpec(memory_space=pltpu.VMEM)],
        out_specs=pl.BlockSpec(memory_space=pltpu.HBM),
        scratch_shapes=[
            pltpu.VMEM((steps, 2, count, count), jnp.float32),
            pltpu.SemaphoreType.DMA((steps, 2)),
        ],
        compiler_params=pltpu.CompilerParams(vmem_limit_bytes=30 << 20),
        cost_estimate=pl.CostEstimate(
            flops=4 * steps * count * count * width,
            bytes_accessed=8 * steps * count * count,
            transcendentals=0,
        ),
    )(received)


def on_device(voltages, filter_taps):
    dumps = lax.axis_size("tm")
    sources = lax.axis_size("inputs")
    table = jnp.asarray(fourier_rows(sources, dumps))
    tail = voltages[:, voltages.shape[1] - (TAPS - 1) * NFFT :]
    halo = lax.ppermute(tail, "tm", [(i, (i + 1) % dumps) for i in range(dumps)])
    spec, filt, head = early(
        pltpu.with_memory_space_constraint(voltages, pltpu.HBM),
        pltpu.with_memory_space_constraint(filter_taps, pltpu.HBM),
        pltpu.with_memory_space_constraint(table, pltpu.HBM),
    )
    spectra = late(halo, head, filter_taps, table, filt, spec)
    moved = lax.all_to_all(spectra, ("inputs", "tm"), split_axis=0, concat_axis=0, tiled=True)
    received = moved.reshape(
        sources, dumps, moved.shape[0] // (dumps * sources), moved.shape[1], moved.shape[2]
    )
    return correlate(received)


def solution(mesh):
    in_specs = (P("inputs", "tm"), P())
    out_specs = P(None, ("tm", "inputs"), None, None, None)
    return jax.shard_map(
        on_device, mesh=mesh, in_specs=in_specs, out_specs=out_specs, check_vma=False
    )
```

```python
import functools
import math

import jax
import jax.numpy as jnp
import ml_dtypes
import numpy as np
from jax import lax
from jax.experimental import pallas as pl
from jax.experimental.pallas import tpu as pltpu
from jax.sharding import PartitionSpec as P

NFFT = 512
TAPS = 4
CHANNELS = NFFT // 2
LANES = 128
GROUP = 16
PAIR = 2
FIRST_UNROLL = 2
BOTH_UNROLL = 2
LATE_UNROLL = 8
REST_UNROLL = 4
TIME = ("yh", "core")
INPUTS = ("z", "yl", "x")
PEERS = ("yl", "z", "x", "core", "yh")
ROWS_BY_ROWS = (((1,), (1,)), ((), ()))


def fourier_rows(places):
    n = np.arange(NFFT)
    k = np.arange(CHANNELS).reshape(places.size, -1)[places.reshape(-1)].reshape(-1)
    phase = (k[:, None] * n[None, :] % NFFT) * (2.0 * math.pi / NFFT)
    factor = 1.0 / math.sqrt(NFFT)
    rows = np.concatenate([np.cos(phase) * factor, -np.sin(phase) * factor], axis=0)
    return rows.astype(np.float32).astype(ml_dtypes.bfloat16)


def filter_group(samples_ref, first, past, taps_ref, store):
    inputs = samples_ref.shape[0]
    for lane in range(0, NFFT, LANES):
        taps = [
            jnp.broadcast_to(taps_ref[t : t + 1, lane : lane + LANES], (inputs, LANES))
            for t in range(TAPS)
        ]
        window = [past(t, lane).astype(jnp.float32) for t in range(TAPS - 1)]
        rows = []
        for s in range(GROUP):
            at = pl.multiple_of((first + s) * NFFT + lane, LANES)
            window.append(samples_ref[:, pl.ds(at, LANES)].astype(jnp.float32))
            total = taps[0] * window[0]
            for t in range(1, TAPS):
                total = total + taps[t] * window[t]
            rows.append(total.astype(jnp.bfloat16))
            window = window[1:]
        store(lane, jnp.swapaxes(jnp.stack(rows, axis=0), 0, 1))


def transform(table_ref, rows, out_ref, p):
    spectra = rows.shape[1]
    result = lax.dot_general(
        table_ref[...],
        rows.reshape(PAIR * spectra, NFFT),
        ROWS_BY_ROWS,
        preferred_element_type=jnp.float32,
    ).astype(jnp.bfloat16)
    for i in range(PAIR):
        out_ref[p * PAIR + i] = result[:, i * spectra : (i + 1) * spectra]


def swap_group(spec_ref, out_ref, g, lane):
    first = pl.multiple_of(g * GROUP, GROUP)
    for r in range(2):
        block = spec_ref[:, pl.ds(r * CHANNELS + first, GROUP), :]
        at = lane + r * LANES
        out_ref[pl.ds(first, GROUP), :, at : at + LANES] = jnp.swapaxes(block, 0, 1)


def loop(steps, body, unroll):
    if unroll == steps:
        for i in range(steps):
            body(i)
        return

    @pl.loop(0, steps // unroll)
    def _(i):
        for u in range(unroll):
            body(i * unroll + u)


def early_kernel(
    v_hbm, taps_hbm, table_hbm, spec_ref, filt_ref, head_ref, v_ref, taps_ref, table_ref, late_ref, sems
):
    inputs = v_ref.shape[0]
    groups = v_ref.shape[1] // (GROUP * NFFT)
    half = groups // 2

    def part(g):
        span = pl.ds(pl.multiple_of(g * GROUP * NFFT, LANES), GROUP * NFFT)
        return pltpu.make_async_copy(v_hbm.at[:, span], v_ref.at[:, span], sems.at[g])

    taps_copy = pltpu.make_async_copy(taps_hbm, taps_ref, sems.at[groups])
    table_copy = pltpu.make_async_copy(table_hbm, table_ref, sems.at[groups + 1])
    taps_copy.start()
    for g in range(half - 1, groups):
        part(g).start()
    table_copy.start()
    for g in range(half - 1):
        part(g).start()

    def run(g, target, at):
        first = g * GROUP

        def past(t, lane):
            start = pl.multiple_of((first - (TAPS - 1) + t) * NFFT + lane, LANES)
            return v_ref[:, pl.ds(start, LANES)]

        def store(lane, block):
            target[:, pl.ds(pl.multiple_of(at * GROUP, GROUP), GROUP), lane : lane + LANES] = block

        filter_group(v_ref, first, past, taps_ref, store)

    taps_copy.wait()
    part(half - 1).wait()

    def second_half(i):
        part(half + i).wait()
        run(half + i, late_ref, i)

    loop(groups - half, second_half, FIRST_UNROLL)
    table_copy.wait()
    for g in range(half - 1):
        part(g).wait()
    head_ref[...] = v_ref[:, : GROUP * NFFT]

    def both(p):
        rows = late_ref[pl.ds(p * PAIR, PAIR)]
        transform(table_ref, rows, spec_ref, p)
        run(jnp.maximum(p, 1), filt_ref, jnp.maximum(p, 1))

    loop(inputs // PAIR, both, BOTH_UNROLL)


def early(voltages, taps, table):
    inputs, samples = voltages.shape
    spectra = samples // NFFT
    any_spec = pl.BlockSpec(memory_space=pltpu.HBM)
    vmem_spec = pl.BlockSpec(memory_space=pltpu.VMEM)
    return pl.pallas_call(
        early_kernel,
        name="early",
        out_shape=(
            jax.ShapeDtypeStruct((inputs, NFFT, spectra // 2), jnp.bfloat16),
            jax.ShapeDtypeStruct((inputs, spectra // 2, NFFT), jnp.bfloat16),
            jax.ShapeDtypeStruct((inputs, GROUP * NFFT), jnp.bfloat16),
        ),
        in_specs=[any_spec] * 3,
        out_specs=(vmem_spec,) * 3,
        scratch_shapes=[
            pltpu.VMEM(voltages.shape, jnp.bfloat16),
            pltpu.VMEM(taps.shape, jnp.float32),
            pltpu.VMEM(table.shape, jnp.bfloat16),
            pltpu.VMEM((inputs, spectra // 2, NFFT), jnp.bfloat16),
            pltpu.SemaphoreType.DMA((2 + spectra // GROUP,)),
        ],
        compiler_params=pltpu.CompilerParams(vmem_limit_bytes=24 << 20),
        cost_estimate=pl.CostEstimate(
            flops=inputs * samples * NFFT, bytes_accessed=2 * inputs * samples, transcendentals=0
        ),
    )(voltages, taps, table)


def late_kernel(halo_ref, head_ref, taps_ref, table_ref, filt_ref, early_ref, out_ref, first_ref, spec_ref):
    inputs = head_ref.shape[0]
    started = lax.axis_index(TIME) > 0

    def past(t, lane):
        block = halo_ref[:, t * NFFT + lane : t * NFFT + lane + LANES].astype(jnp.float32)
        return jnp.where(started, block, 0.0)

    def store(lane, block):
        first_ref[:, :, lane : lane + LANES] = block

    filter_group(head_ref, 0, past, taps_ref, store)
    pairs = inputs // PAIR
    groups = CHANNELS // GROUP

    def both(p):
        pair = pl.ds(p * PAIR, PAIR)
        rows = jnp.concatenate([first_ref[pair], filt_ref[pair, GROUP:, :]], axis=1)
        transform(table_ref, rows, spec_ref, p)
        for q in range(groups // pairs):
            swap_group(early_ref, out_ref, p * (groups // pairs) + q, 2 * LANES)

    loop(pairs, both, LATE_UNROLL)

    def rest(g):
        swap_group(spec_ref, out_ref, g, 0)

    loop(groups, rest, REST_UNROLL)


def late(halo, head, taps, table, filt, spec):
    inputs, spectra, _ = filt.shape
    vmem_spec = pl.BlockSpec(memory_space=pltpu.VMEM)
    return pl.pallas_call(
        late_kernel,
        name="late",
        out_shape=jax.ShapeDtypeStruct((CHANNELS, inputs, 4 * spectra), jnp.bfloat16),
        in_specs=[vmem_spec] * 6,
        out_specs=vmem_spec,
        scratch_shapes=[
            pltpu.VMEM((inputs, GROUP, NFFT), jnp.bfloat16),
            pltpu.VMEM((inputs, NFFT, spectra), jnp.bfloat16),
        ],
        compiler_params=pltpu.CompilerParams(vmem_limit_bytes=20 << 20),
        cost_estimate=pl.CostEstimate(
            flops=2 * inputs * spectra * NFFT * NFFT,
            bytes_accessed=4 * inputs * spectra * NFFT,
            transcendentals=0,
        ),
    )(halo, head, taps, table, filt, spec)


def correlate_kernel(slots, x_ref, out_hbm, out_ref, sems):
    dumps, sources = slots.shape
    _, channels, inputs, width = x_ref.shape
    scale = 2.0 / width
    copies = []

    def send(step, part):
        target = out_hbm.at[step // channels, step % channels, part]
        copies.append(pltpu.make_async_copy(out_ref.at[step, part], target, sems.at[step, part]))
        copies[-1].start()

    for step in range(dumps * channels):
        x = jnp.concatenate(
            [x_ref[int(slot), step % channels] for slot in slots[step // channels]], axis=0
        )
        real = lax.dot_general(x, x, ROWS_BY_ROWS, preferred_element_type=jnp.float32)
        out_ref[step, 0] = real * scale
        send(step, 0)
        turned = []
        for at in range(0, width, 2 * LANES):
            turned += [x[:, at + LANES : at + 2 * LANES], -x[:, at : at + LANES]]
        imag = lax.dot_general(
            jnp.concatenate(turned, axis=1), x, ROWS_BY_ROWS, preferred_element_type=jnp.float32
        )
        out_ref[step, 1] = imag * scale
        send(step, 1)
    for copy in copies:
        copy.wait()


def correlate(received, slots):
    dumps, sources = slots.shape
    _, channels, inputs, width = received.shape
    count = sources * inputs
    steps = dumps * channels
    return pl.pallas_call(
        functools.partial(correlate_kernel, slots),
        name="correlate",
        out_shape=jax.ShapeDtypeStruct((dumps, channels, 2, count, count), jnp.float32),
        in_specs=[pl.BlockSpec(memory_space=pltpu.VMEM)],
        out_specs=pl.BlockSpec(memory_space=pltpu.HBM),
        scratch_shapes=[
            pltpu.VMEM((steps, 2, count, count), jnp.float32),
            pltpu.SemaphoreType.DMA((steps, 2)),
        ],
        compiler_params=pltpu.CompilerParams(vmem_limit_bytes=30 << 20),
        cost_estimate=pl.CostEstimate(
            flops=4 * steps * count * count * width,
            bytes_accessed=8 * steps * count * count,
            transcendentals=0,
        ),
    )(received)


def on_device(voltages, filter_taps, places):
    dumps = lax.axis_size(TIME)
    table = jnp.asarray(fourier_rows(places))
    tail = voltages[:, voltages.shape[1] - (TAPS - 1) * NFFT :]
    halo = lax.ppermute(tail, TIME, [(i, (i + 1) % dumps) for i in range(dumps)])
    spec, filt, head = early(
        pltpu.with_memory_space_constraint(voltages, pltpu.HBM),
        pltpu.with_memory_space_constraint(filter_taps, pltpu.HBM),
        pltpu.with_memory_space_constraint(table, pltpu.HBM),
    )
    spectra = late(halo, head, filter_taps, table, filt, spec)
    moved = lax.all_to_all(spectra, PEERS, split_axis=0, concat_axis=0, tiled=True)
    received = moved.reshape(places.size, -1, moved.shape[1], moved.shape[2])
    return correlate(received, np.argsort(places.reshape(-1)).reshape(dumps, -1))


def solution(mesh):
    sizes = dict(yh=2, core=2, z=4, yl=2, x=4)
    names = TIME + INPUTS
    assert mesh.devices.size == math.prod(sizes.values())
    fine = jax.sharding.Mesh(mesh.devices.reshape([sizes[n] for n in names]), names)
    places = np.arange(mesh.devices.size).reshape([sizes[n] for n in names])
    places = places.transpose([names.index(n) for n in PEERS])
    return jax.shard_map(
        functools.partial(on_device, places=places),
        mesh=fine,
        in_specs=(P(INPUTS, TIME), P()),
        out_specs=P(None, names, None, None, None),
        check_vma=False,
    )
```

```python
import functools
import math

import jax
import jax.numpy as jnp
import ml_dtypes
import numpy as np
from jax import lax
from jax.experimental import pallas as pl
from jax.experimental.pallas import tpu as pltpu
from jax.sharding import PartitionSpec as P

NFFT = 512
TAPS = 4
CHANNELS = NFFT // 2
LANES = 128
GROUP = 16
PAIR = 2
FIRST_UNROLL = 1
BOTH_UNROLL = 2
LATE_UNROLL = 8
REST_UNROLL = 2
TIME = ("yh", "core")
INPUTS = ("z", "yl", "x")
PEERS = ("yl", "z", "x", "core", "yh")
ROWS_BY_ROWS = (((1,), (1,)), ((), ()))


def fourier_rows(places):
    n = np.arange(NFFT)
    k = np.arange(CHANNELS).reshape(places.size, -1)[places.reshape(-1)].reshape(-1)
    phase = (k[:, None] * n[None, :] % NFFT) * (2.0 * math.pi / NFFT)
    factor = 1.0 / math.sqrt(NFFT)
    rows = np.concatenate([np.cos(phase) * factor, -np.sin(phase) * factor], axis=0)
    return rows.astype(np.float32).astype(ml_dtypes.bfloat16)


def filter_group(samples_ref, first, past, taps_ref, store):
    inputs = samples_ref.shape[0]
    for lane in range(0, NFFT, LANES):
        taps = [
            jnp.broadcast_to(taps_ref[t : t + 1, lane : lane + LANES], (inputs, LANES))
            for t in range(TAPS)
        ]
        window = [past(t, lane).astype(jnp.float32) for t in range(TAPS - 1)]
        rows = []
        for s in range(GROUP):
            at = pl.multiple_of((first + s) * NFFT + lane, LANES)
            window.append(samples_ref[:, pl.ds(at, LANES)].astype(jnp.float32))
            total = taps[0] * window[0]
            for t in range(1, TAPS):
                total = total + taps[t] * window[t]
            rows.append(total.astype(jnp.bfloat16))
            window = window[1:]
        store(lane, jnp.swapaxes(jnp.stack(rows, axis=0), 0, 1))


def transform(table_ref, rows, out_ref, p):
    spectra = rows.shape[1]
    result = lax.dot_general(
        table_ref[...],
        rows.reshape(PAIR * spectra, NFFT),
        ROWS_BY_ROWS,
        preferred_element_type=jnp.float32,
    ).astype(jnp.bfloat16)
    for i in range(PAIR):
        out_ref[p * PAIR + i] = result[:, i * spectra : (i + 1) * spectra]


def swap_group(spec_ref, out_ref, g, lane):
    first = pl.multiple_of(g * GROUP, GROUP)
    for r in range(2):
        block = spec_ref[:, pl.ds(r * CHANNELS + first, GROUP), :]
        at = lane + r * LANES
        out_ref[pl.ds(first, GROUP), :, at : at + LANES] = jnp.swapaxes(block, 0, 1)


def loop(steps, body, unroll):
    if unroll == steps:
        for i in range(steps):
            body(i)
        return

    @pl.loop(0, steps // unroll)
    def _(i):
        for u in range(unroll):
            body(i * unroll + u)


def early_kernel(
    v_hbm, taps_hbm, table_hbm, spec_ref, filt_ref, head_ref, v_ref, taps_ref, table_ref, late_ref, sems
):
    inputs = v_ref.shape[0]
    groups = v_ref.shape[1] // (GROUP * NFFT)
    half = groups // 2

    def part(g):
        span = pl.ds(pl.multiple_of(g * GROUP * NFFT, LANES), GROUP * NFFT)
        return pltpu.make_async_copy(v_hbm.at[:, span], v_ref.at[:, span], sems.at[g])

    taps_copy = pltpu.make_async_copy(taps_hbm, taps_ref, sems.at[groups])
    table_copy = pltpu.make_async_copy(table_hbm, table_ref, sems.at[groups + 1])
    taps_copy.start()
    for g in range(half - 1, groups):
        part(g).start()
    table_copy.start()
    for g in range(half - 1):
        part(g).start()

    def run(g, target, at):
        first = g * GROUP

        def past(t, lane):
            start = pl.multiple_of((first - (TAPS - 1) + t) * NFFT + lane, LANES)
            return v_ref[:, pl.ds(start, LANES)]

        def store(lane, block):
            target[:, pl.ds(pl.multiple_of(at * GROUP, GROUP), GROUP), lane : lane + LANES] = block

        filter_group(v_ref, first, past, taps_ref, store)

    taps_copy.wait()
    part(half - 1).wait()

    def second_half(i):
        part(half + i).wait()
        run(half + i, late_ref, i)

    loop(groups - half, second_half, FIRST_UNROLL)
    table_copy.wait()
    for g in range(half - 1):
        part(g).wait()
    head_ref[...] = v_ref[:, : GROUP * NFFT]

    def both(p):
        rows = late_ref[pl.ds(p * PAIR, PAIR)]
        transform(table_ref, rows, spec_ref, p)
        run(jnp.maximum(p, 1), filt_ref, jnp.maximum(p, 1))

    loop(inputs // PAIR, both, BOTH_UNROLL)


def early(voltages, taps, table):
    inputs, samples = voltages.shape
    spectra = samples // NFFT
    any_spec = pl.BlockSpec(memory_space=pltpu.HBM)
    vmem_spec = pl.BlockSpec(memory_space=pltpu.VMEM)
    return pl.pallas_call(
        early_kernel,
        name="early",
        out_shape=(
            jax.ShapeDtypeStruct((inputs, NFFT, spectra // 2), jnp.bfloat16),
            jax.ShapeDtypeStruct((inputs, spectra // 2, NFFT), jnp.bfloat16),
            jax.ShapeDtypeStruct((inputs, GROUP * NFFT), jnp.bfloat16),
        ),
        in_specs=[any_spec] * 3,
        out_specs=(vmem_spec,) * 3,
        scratch_shapes=[
            pltpu.VMEM(voltages.shape, jnp.bfloat16),
            pltpu.VMEM(taps.shape, jnp.float32),
            pltpu.VMEM(table.shape, jnp.bfloat16),
            pltpu.VMEM((inputs, spectra // 2, NFFT), jnp.bfloat16),
            pltpu.SemaphoreType.DMA((2 + spectra // GROUP,)),
        ],
        compiler_params=pltpu.CompilerParams(vmem_limit_bytes=24 << 20),
        cost_estimate=pl.CostEstimate(
            flops=inputs * samples * NFFT, bytes_accessed=2 * inputs * samples, transcendentals=0
        ),
    )(voltages, taps, table)


def late_kernel(halo_ref, head_ref, taps_ref, table_ref, filt_ref, early_ref, out_ref, first_ref, spec_ref):
    inputs = head_ref.shape[0]
    started = lax.axis_index(TIME) > 0

    def past(t, lane):
        block = halo_ref[:, t * NFFT + lane : t * NFFT + lane + LANES].astype(jnp.float32)
        return jnp.where(started, block, 0.0)

    def store(lane, block):
        first_ref[:, :, lane : lane + LANES] = block

    filter_group(head_ref, 0, past, taps_ref, store)
    pairs = inputs // PAIR
    groups = CHANNELS // GROUP

    def both(p):
        pair = pl.ds(p * PAIR, PAIR)
        rows = jnp.concatenate([first_ref[pair], filt_ref[pair, GROUP:, :]], axis=1)
        transform(table_ref, rows, spec_ref, p)
        for q in range(groups // pairs):
            swap_group(early_ref, out_ref, p * (groups // pairs) + q, 2 * LANES)

    loop(pairs, both, LATE_UNROLL)

    def rest(g):
        swap_group(spec_ref, out_ref, g, 0)

    loop(groups, rest, REST_UNROLL)


def late(halo, head, taps, table, filt, spec):
    inputs, spectra, _ = filt.shape
    vmem_spec = pl.BlockSpec(memory_space=pltpu.VMEM)
    return pl.pallas_call(
        late_kernel,
        name="late",
        out_shape=jax.ShapeDtypeStruct((CHANNELS, inputs, 4 * spectra), jnp.bfloat16),
        in_specs=[vmem_spec] * 6,
        out_specs=vmem_spec,
        scratch_shapes=[
            pltpu.VMEM((inputs, GROUP, NFFT), jnp.bfloat16),
            pltpu.VMEM((inputs, NFFT, spectra), jnp.bfloat16),
        ],
        compiler_params=pltpu.CompilerParams(vmem_limit_bytes=20 << 20),
        cost_estimate=pl.CostEstimate(
            flops=2 * inputs * spectra * NFFT * NFFT,
            bytes_accessed=4 * inputs * spectra * NFFT,
            transcendentals=0,
        ),
    )(halo, head, taps, table, filt, spec)


def correlate_kernel(slots, x_ref, out_hbm, out_ref, sems):
    dumps, sources = slots.shape
    _, channels, inputs, width = x_ref.shape
    scale = 2.0 / width
    copies = []

    def send(step, part):
        target = out_hbm.at[step // channels, step % channels, part]
        copies.append(pltpu.make_async_copy(out_ref.at[step, part], target, sems.at[step, part]))
        copies[-1].start()

    for step in range(dumps * channels):
        x = jnp.concatenate(
            [x_ref[int(slot), step % channels] for slot in slots[step // channels]], axis=0
        )
        real = lax.dot_general(x, x, ROWS_BY_ROWS, preferred_element_type=jnp.float32)
        out_ref[step, 0] = real * scale
        send(step, 0)
        turned = []
        for at in range(0, width, 2 * LANES):
            turned += [x[:, at + LANES : at + 2 * LANES], -x[:, at : at + LANES]]
        imag = lax.dot_general(
            jnp.concatenate(turned, axis=1), x, ROWS_BY_ROWS, preferred_element_type=jnp.float32
        )
        out_ref[step, 1] = imag * scale
        send(step, 1)
    for copy in copies:
        copy.wait()


def correlate(received, slots):
    dumps, sources = slots.shape
    _, channels, inputs, width = received.shape
    count = sources * inputs
    steps = dumps * channels
    return pl.pallas_call(
        functools.partial(correlate_kernel, slots),
        name="correlate",
        out_shape=jax.ShapeDtypeStruct((dumps, channels, 2, count, count), jnp.float32),
        in_specs=[pl.BlockSpec(memory_space=pltpu.VMEM)],
        out_specs=pl.BlockSpec(memory_space=pltpu.HBM),
        scratch_shapes=[
            pltpu.VMEM((steps, 2, count, count), jnp.float32),
            pltpu.SemaphoreType.DMA((steps, 2)),
        ],
        compiler_params=pltpu.CompilerParams(vmem_limit_bytes=30 << 20),
        cost_estimate=pl.CostEstimate(
            flops=4 * steps * count * count * width,
            bytes_accessed=8 * steps * count * count,
            transcendentals=0,
        ),
    )(received)


def on_device(voltages, filter_taps, places):
    dumps = lax.axis_size(TIME)
    table = jnp.asarray(fourier_rows(places))
    tail = voltages[:, voltages.shape[1] - (TAPS - 1) * NFFT :]
    halo = lax.ppermute(tail, TIME, [(i, (i + 1) % dumps) for i in range(dumps)])
    spec, filt, head = early(
        pltpu.with_memory_space_constraint(voltages, pltpu.HBM),
        pltpu.with_memory_space_constraint(filter_taps, pltpu.HBM),
        pltpu.with_memory_space_constraint(table, pltpu.HBM),
    )
    spectra = late(halo, head, filter_taps, table, filt, spec)
    moved = lax.all_to_all(spectra, PEERS, split_axis=0, concat_axis=0, tiled=True)
    received = moved.reshape(places.size, -1, moved.shape[1], moved.shape[2])
    return correlate(received, np.argsort(places.reshape(-1)).reshape(dumps, -1))


def solution(mesh):
    sizes = dict(yh=2, core=2, z=4, yl=2, x=4)
    names = TIME + INPUTS
    assert mesh.devices.size == math.prod(sizes.values())
    fine = jax.sharding.Mesh(mesh.devices.reshape([sizes[n] for n in names]), names)
    places = np.arange(mesh.devices.size).reshape([sizes[n] for n in names])
    places = places.transpose([names.index(n) for n in PEERS])
    return jax.shard_map(
        functools.partial(on_device, places=places),
        mesh=fine,
        in_specs=(P(INPUTS, TIME), P()),
        out_specs=P(None, names, None, None, None),
        check_vma=False,
    )
```
